32 devices in a mesh: gx: 4 (over z), gy: 2 (over x), gz: 4 (over y, core).
Axes of the slice: x: 2, y: 2, z: 4, core: 2. Of those that a mesh axis runs over, the one named last changes fastest.
Arguments:
- positions: float32 [3, 16384], P(None, ('gx', 'gy', 'gz')), may hold values from -6 to 6
- frames: float32 [128, 3, 4096], P(None, None, ('gy', 'gz')), may hold values from -6 to 6
- path_slot: int32 [32, 512], P(('gx', 'gy', 'gz')), may hold values from 0 to 511, as said below
- path_count: int32 [32], replicated, may hold values from 1 to 512, 4096 in all
- path_order: int32 [4096], replicated, may hold values from 0 to 4095, each once
- frame_rank: int32 [128], replicated, may hold values from 0 to 127, each once
Outputs:
- forces: float32 [3, 16384], P(None, ('gx', 'gy', 'gz'))
- path_cv: float32 [2], replicated
The draws below stay inside these ranges and needn't reach their ends.
Inputs may be any that keep to these rules, and one draw needn't show every extreme that they name: `path_slot`: within one domain's row the 512 local atom indices are all different.
All inputs are finite; a program needn't handle non-finite values.
Results may differ from the reference program's by a relative error of at most 0.00013.
Values sent between devices are 32-bit elements; how exact they have to be, the bound alone decides.
A program may use at most 64 MiB of HBM per device.

```python
import math
import jax
import jax.numpy as jnp
import numpy as np
from jax import lax

P_SIZE = 4096
F = 128
ATOM_DEV = 512
SLOTS = 512
ATOMS = 16384
DEVICES = 32


def draw_path_slot(key, part):
    keys = jax.random.split(jax.random.fold_in(key, 17), DEVICES)
    rows = jax.vmap(lambda k: jax.random.permutation(k, ATOM_DEV)[:SLOTS])(keys)
    return rows.astype(jnp.int32)


def levels(rng, extent, cuts, low, largest):
    gain, own = 1.0, jax.random.fold_in(rng, 6)
    for dim, blocks in cuts:
        steps = jnp.exp(jax.random.uniform(jax.random.fold_in(own, dim), (blocks,), jnp.float32, low / len(cuts), largest / len(cuts)))
        gain = gain * jnp.repeat(steps, extent[dim] // blocks).reshape([-1 if axis == dim else 1 for axis in range(len(extent))])
    return gain


def split_up(amount, total, limit, lean):
    loads = [(1 << 20) // math.isqrt(grade ** lean) + 1 for grade in range(2, amount + 1)]
    rest, counts = total - limit - (amount - 1), [1] * (amount - 1)
    while rest > 0:
        free = [i for i in range(amount - 1) if counts[i] < limit]
        whole, remaining = sum([loads[i] for i in free]), rest
        for i in free:
            more = min(limit - counts[i], max(1, remaining * loads[i] // whole), rest)
            counts[i] = counts[i] + more
            rest = rest - more
    return np.array([limit] + counts)


def ragged(stream_key, number_of, total, most, slope):
    if number_of == 2:
        one = jax.random.randint(stream_key, (), max(1, total - most), min(most, total - 1) + 1)
        return jnp.stack([one, total - one])
    tallies = jnp.asarray(split_up(number_of, total, most, slope), jnp.int32)
    couples = (number_of - 1) // 2
    source_of, taker = tallies[1:1 + 2 * couples:2], tallies[2:2 + 2 * couples:2]
    room = jnp.minimum(source_of - 1, most - taker)
    shifted = jax.random.randint(jax.random.fold_in(stream_key, 1), (couples,), 0, 1 << 20) % (room + 1)
    tallies = tallies.at[1:1 + 2 * couples:2].set(source_of - shifted).at[2:2 + 2 * couples:2].set(taker + shifted)
    return tallies[jax.random.permutation(jax.random.fold_in(stream_key, 2), number_of)]


def centred(stream_key, shape, scale, reach, pieces=(), kind=jnp.bfloat16):
    gain = levels(stream_key, shape, pieces, -0.22, 0.18) if pieces else 1.0
    array = jax.random.normal(stream_key, shape, jnp.float32) * scale * gain
    return jnp.minimum(jnp.maximum(array, -reach), reach).astype(kind)


def setup_inputs(seed: int = 0) -> dict:
    arg_keys = jax.random.split(jax.random.key(seed), 7)
    return {
        "positions": centred(arg_keys[0], (3, ATOMS), 1.0, 6.0, ((1, 32),), jnp.float32),
        "frames": centred(arg_keys[1], (F, 3, P_SIZE), 1.0, 6.0, ((2, 8),), jnp.float32),
        "path_slot": draw_path_slot(jax.random.fold_in(arg_keys[6], 71), 0),
        "path_count": ragged(arg_keys[3], DEVICES, P_SIZE, SLOTS, 2).astype(jnp.int32),
        "path_order": jax.random.permutation(arg_keys[4], P_SIZE).astype(jnp.int32),
        "frame_rank": jax.random.permutation(arg_keys[5], F).astype(jnp.int32),
    }


STRENGTH = 20.0
S_HOME = 0.5
KAPPA_S = 0.5
KAPPA_Z = 0.05
PAIR_SCALE = 0.02
WIDTH_SQ = 4.0


def pair_block(block_pos, all_pos):
    diff = block_pos[:, :, None] - all_pos[:, None, :]
    dist_sq = jnp.sum(diff * diff, axis=0)
    weight = PAIR_SCALE * jnp.exp(-dist_sq / WIDTH_SQ)
    return jnp.sum(weight[None] * diff, axis=2)


def domain_forces(local):
    atoms = local.shape[1]
    rows = 256 if atoms % 256 == 0 else atoms
    blocks = local.reshape(3, atoms // rows, rows).transpose(1, 0, 2)
    result = lax.map(lambda block: pair_block(block, local), blocks)
    return result.transpose(1, 0, 2).reshape(3, atoms)


def slot_ids(path_count, path_order, slots):
    offsets = jnp.cumsum(path_count) - path_count
    steps_k = jnp.arange(slots, dtype=jnp.int32)
    live = steps_k[None, :] < path_count[:, None]
    place = jnp.clip(offsets[:, None] + steps_k[None, :], 0, P_SIZE - 1).astype(jnp.int32)
    ids = jnp.where(live, path_order[place], -1).astype(jnp.int32)
    return ids, live


def cv_terms(dist, frame_rank):
    frames_n = dist.shape[0]
    expo = -STRENGTH * dist
    top = jnp.max(expo)
    expd = jnp.exp(expo - top)
    total = jnp.sum(expd)
    weight = expd / total
    progress_rank = frame_rank.astype(jnp.float32) / (frames_n - 1.0)
    s_value = jnp.sum(progress_rank * weight)
    z_value = -(top + jnp.log(total)) / STRENGTH
    grads = KAPPA_S * P_SIZE * (s_value - S_HOME) * (-STRENGTH) * weight * (progress_rank - s_value) + KAPPA_Z * P_SIZE * z_value * weight
    return s_value, z_value, grads


def reference(positions, frames, path_slot, path_count, path_order, frame_rank):
    domains = path_slot.shape[0]
    slots = path_slot.shape[1]
    ids, live = slot_ids(path_count, path_order, slots)
    atom_index = (jnp.arange(domains, dtype=jnp.int32)[:, None] * ATOM_DEV + path_slot).astype(jnp.int32)
    flat_atoms = atom_index.reshape(-1)
    flat_ids = jnp.clip(ids.reshape(-1), 0, P_SIZE - 1).astype(jnp.int32)
    mask = live.reshape(-1).astype(jnp.float32)
    path_pos = positions[:, flat_atoms]
    refs = frames[:, :, flat_ids]
    delta = path_pos[None] - refs
    dist = jnp.sum(jnp.sum(delta * delta, axis=1) * mask[None], axis=1) / P_SIZE
    s_value, z_value, grads = cv_terms(dist, frame_rank)
    bias = -(2.0 / P_SIZE) * jnp.einsum('f,fcm->cm', grads, delta, precision=lax.Precision.HIGHEST) * mask[None]
    local = positions.reshape(3, domains, ATOM_DEV).transpose(1, 0, 2)
    pair = lax.map(domain_forces, local)
    forces = pair.transpose(1, 0, 2).reshape(3, domains * ATOM_DEV)
    forces = forces.at[:, flat_atoms].add(bias)
    return forces, jnp.stack([s_value, z_value])
```

```python
import functools

import jax
import jax.numpy as jnp
from jax import lax
from jax.experimental import pallas as pl
from jax.experimental.pallas import tpu as pltpu
from jax.sharding import PartitionSpec as P

STRENGTH = 20.0
S_HOME = 0.5
KAPPA_S = 0.5
KAPPA_Z = 0.05
PAIR_SCALE = 0.02
WIDTH_SQ = 4.0
LANES = 128
MESH = pl.DeviceIdType.MESH
NT = (((1,), (1,)), ((), ()))
NN = (((1,), (0,)), ((), ()))


def three_parts(x):
    high = x.astype(jnp.bfloat16).astype(jnp.float32)
    rest = x - high
    middle = rest.astype(jnp.bfloat16).astype(jnp.float32)
    return high, middle, rest - middle


def dot(a, b, dims):
    return lax.dot_general(
        a.astype(jnp.bfloat16), b.astype(jnp.bfloat16), dims, preferred_element_type=jnp.float32
    )


def iota(shape, axis):
    return lax.broadcasted_iota(jnp.int32, shape, axis)


def kernel(
    sizes, tile, cpad,
    pos_ref, frames_hbm, slot_ref, count_ref, order_ref, rank_ref,
    force_ref, cv_ref,
    frames, out1, in1, all2, all3, pair, cols, frames_sem, send1, recv1, send2, recv2, send3, recv3,
):
    nx, ny, nz = sizes
    plane = ny * nz
    n = nx * plane
    atoms = pos_ref.shape[1]
    slots = slot_ref.shape[1]
    order_rows = order_ref.shape[0]
    path = order_rows * LANES
    frames_n = frames.shape[1]
    block = frames.shape[2]
    parts = block // tile
    gx, gy, gz = lax.axis_index("gx"), lax.axis_index("gy"), lax.axis_index("gz")
    here = gy * nz + gz
    me = gx * plane + here

    def peer_of(step):
        other = lax.rem(me + step, n)
        row = lax.rem(other, plane)
        return other, (other // plane, row // nz, lax.rem(row, nz))

    def plane_peer(step):
        row = lax.rem(here + step, plane)
        return row, (gx, row // nz, lax.rem(row, nz))

    def loop(count, fn):
        lax.fori_loop(1, count, lambda step, _: (fn(step), 0)[1], 0, unroll=count <= 64)

    fetch = pltpu.make_async_copy(frames_hbm, frames, frames_sem)
    fetch.start()

    barrier = pltpu.get_barrier_semaphore()

    def greet(step):
        pl.semaphore_signal(barrier, inc=1, device_id=peer_of(step)[1], device_id_type=MESH)

    loop(n, greet)

    counts = count_ref[...]
    lane_n = iota(counts.shape, 1)
    offset = jnp.sum(jnp.where(lane_n < me, counts, 0).astype(jnp.float32), axis=1, keepdims=True).astype(jnp.int32)
    mine = jnp.sum(jnp.where(lane_n == me, counts, 0).astype(jnp.float32), axis=1, keepdims=True).astype(jnp.int32)
    k = iota((1, slots), 1)
    place = k + offset
    live_k = (k < mine).astype(jnp.float32)
    order = order_ref[...]
    table = jnp.concatenate([order // tile, lax.rem(order, tile)], axis=0).astype(jnp.float32)
    column = (iota((LANES, slots), 0) == lax.rem(place, LANES)).astype(jnp.float32)
    picked = dot(table, column, NN)
    row_hit = iota((order_rows, slots), 0) == place // LANES
    high_k = jnp.sum(jnp.where(row_hit, picked[:order_rows], 0.0), axis=0, keepdims=True)
    low_k = jnp.sum(jnp.where(row_hit, picked[order_rows:], 0.0), axis=0, keepdims=True)
    triple = jnp.concatenate(
        [high_k * live_k, low_k * live_k, live_k, jnp.zeros((5, slots), jnp.float32)], axis=0
    )
    slot_hit = (iota((atoms, slots), 0) == slot_ref[...]).astype(jnp.float32)
    per_atom = dot(triple, slot_hit, NT)
    live = per_atom[2:3]
    high = jnp.where(live > 0.5, per_atom[0:1].astype(jnp.int32), -1)
    low = per_atom[1:2].astype(jnp.int32)
    low_hit = (iota((tile, atoms), 0) == low).astype(jnp.bfloat16)

    pos = pos_ref[...]
    blocks = path // tile
    rows = blocks * cpad
    group = [pos, live]
    if cpad > 4:
        group.append(jnp.zeros((cpad - 4, atoms), jnp.float32))
    else:
        group = group * 2
    eight = jnp.concatenate(group, axis=0)
    high_hit = (iota((rows, atoms), 0) // cpad) == high
    sent = jnp.zeros((rows, tile), jnp.float32)
    for piece in three_parts(eight):
        wide = jnp.broadcast_to(piece[None], (rows // 8, 8, atoms)).reshape(rows, atoms)
        sent = sent + dot(jnp.where(high_hit, wide, 0.0), low_hit, NT)
    out1[...] = sent.reshape(plane, parts * cpad, tile)

    pl.semaphore_wait(barrier, n - 1)

    def copy1(step):
        row, device = plane_peer(step)
        return pltpu.make_async_remote_copy(
            src_ref=out1.at[row], dst_ref=in1.at[here], send_sem=send1.at[row], recv_sem=recv1.at[here],
            device_id=device, device_id_type=MESH)

    def landed1(step):
        row, device = plane_peer(step)
        pltpu.make_async_remote_copy(
            src_ref=out1.at[row], dst_ref=in1.at[row], send_sem=send1.at[row], recv_sem=recv1.at[row],
            device_id=device, device_id_type=MESH).wait_recv()

    loop(plane, lambda step: copy1(step).start())
    in1[here] = out1[here]

    height = min(32, atoms)
    padded = jnp.concatenate([pos, jnp.zeros((5, atoms), jnp.float32)], axis=0)
    cols[...] = padded.T

    def pair_step(step, totals):
        at = pl.multiple_of(step * height, height)
        source = cols[pl.ds(at, height), :]
        diffs = [pos[c:c + 1] - source[:, c:c + 1] for c in range(3)]
        dist_sq = diffs[0] * diffs[0] + diffs[1] * diffs[1] + diffs[2] * diffs[2]
        weight = PAIR_SCALE * jnp.exp(-dist_sq / WIDTH_SQ)
        return tuple(
            total + jnp.sum((weight * diff).reshape(height // 8, 8, atoms), axis=0)
            for total, diff in zip(totals, diffs)
        )

    steps = atoms // height
    first = steps // 2
    totals = lax.fori_loop(0, first, pair_step, (jnp.zeros((8, atoms), jnp.float32),) * 3)

    loop(plane, landed1)
    fetch.wait()
    known = jnp.sum(in1[...], axis=0)
    squares = jnp.zeros((frames_n, tile), jnp.float32)
    for t in range(parts):
        part = jnp.zeros((frames_n, tile), jnp.float32)
        for c in range(3):
            row = t * cpad + c
            delta = known[row:row + 1] - frames[c, :, t * tile:(t + 1) * tile]
            part = part + delta * delta
        squares = squares + part * known[t * cpad + 3:t * cpad + 4]
    all2[me] = jnp.sum(squares.T, axis=0, keepdims=True)

    def copy2(step):
        other, device = peer_of(step)
        return pltpu.make_async_remote_copy(
            src_ref=all2.at[me], dst_ref=all2.at[me], send_sem=send2.at[other], recv_sem=recv2.at[me],
            device_id=device, device_id_type=MESH)

    def landed2(step):
        other, device = peer_of(step)
        pltpu.make_async_remote_copy(
            src_ref=all2.at[other], dst_ref=all2.at[other], send_sem=send2.at[other], recv_sem=recv2.at[other],
            device_id=device, device_id_type=MESH).wait_recv()

    loop(n, lambda step: copy2(step).start())

    totals = lax.fori_loop(first, steps, pair_step, totals)
    pair[...] = jnp.concatenate([jnp.sum(total, axis=0, keepdims=True) for total in totals], axis=0)

    loop(n, landed2)
    dist = jnp.sum(all2[...], axis=0) / path
    expo = -STRENGTH * dist
    top = jnp.max(expo, axis=1, keepdims=True)
    expd = jnp.exp(expo - top)
    total = jnp.sum(expd, axis=1, keepdims=True)
    weight = expd / total
    progress = rank_ref[...].astype(jnp.float32) / (frames_n - 1.0)
    s_value = jnp.sum(progress * weight, axis=1, keepdims=True)
    z_value = -(top + jnp.log(total)) / STRENGTH
    grads = (
        KAPPA_S * path * (s_value - S_HOME) * -STRENGTH * weight * (progress - s_value)
        + KAPPA_Z * path * z_value * weight
    )
    cv_ref[...] = jnp.concatenate([s_value, z_value], axis=1)
    down = jnp.broadcast_to(grads, (tile, frames_n)).T
    moved = []
    for t in range(parts):
        for c in range(3):
            moved.append(jnp.sum(down * frames[c, :, t * tile:(t + 1) * tile], axis=0, keepdims=True))
        moved.append(jnp.zeros((cpad - 3, tile), jnp.float32))
    all3[here] = jnp.concatenate(moved, axis=0)

    def copy3(step):
        row, device = plane_peer(step)
        return pltpu.make_async_remote_copy(
            src_ref=all3.at[here], dst_ref=all3.at[here], send_sem=send3.at[row], recv_sem=recv3.at[here],
            device_id=device, device_id_type=MESH)

    def landed3(step):
        row, device = plane_peer(step)
        pltpu.make_async_remote_copy(
            src_ref=all3.at[row], dst_ref=all3.at[row], send_sem=send3.at[row], recv_sem=recv3.at[row],
            device_id=device, device_id_type=MESH).wait_recv()

    loop(plane, lambda step: copy3(step).start())
    loop(plane, lambda step: copy1(step).wait_send())
    loop(n, lambda step: copy2(step).wait_send())
    grads_sum = jnp.sum(grads, axis=1, keepdims=True)
    loop(plane, landed3)
    full = all3[...].reshape(rows, tile)
    spread = jnp.zeros((rows, atoms), jnp.float32)
    for piece in three_parts(full):
        spread = spread + dot(piece, low_hit, NN)
    chosen = jnp.sum(jnp.where(high_hit, spread, 0.0).reshape(rows // 8, 8, atoms), axis=0)
    mean_ref = chosen[0:3]
    if cpad == 4:
        mean_ref = mean_ref + chosen[4:7]
    bias = -(2.0 / path) * (grads_sum * pos - mean_ref) * live
    force_ref[...] = pair[...] + bias
    loop(plane, lambda step: copy3(step).wait_send())


def solution(mesh):
    sizes = tuple(mesh.shape[name] for name in ("gx", "gy", "gz"))

    def body(positions, frames, path_slot, path_count, path_order, frame_rank):
        plane = sizes[1] * sizes[2]
        n = sizes[0] * plane
        atoms = positions.shape[1]
        frames_n, _, block = frames.shape
        tile = min(LANES, block)
        parts = block // tile
        cpad = 4 if parts % 2 == 0 else 8
        dma = pltpu.SemaphoreType.DMA
        vmem = pl.BlockSpec(memory_space=pltpu.VMEM)
        forces, cv = pl.pallas_call(
            functools.partial(kernel, sizes, tile, cpad),
            out_shape=(
                jax.ShapeDtypeStruct((3, atoms), jnp.float32),
                jax.ShapeDtypeStruct((1, 2), jnp.float32),
            ),
            in_specs=[vmem, pl.BlockSpec(memory_space=pl.ANY), vmem, vmem, vmem, vmem],
            out_specs=(vmem, vmem),
            scratch_shapes=[
                pltpu.VMEM((3, frames_n, block), jnp.float32),
                pltpu.VMEM((plane, parts * cpad, tile), jnp.float32),
                pltpu.VMEM((plane, parts * cpad, tile), jnp.float32),
                pltpu.VMEM((n, 1, frames_n), jnp.float32),
                pltpu.VMEM((plane, parts * cpad, tile), jnp.float32),
                pltpu.VMEM((3, atoms), jnp.float32),
                pltpu.VMEM((atoms, 8), jnp.float32),
                dma,
                dma((plane,)), dma((plane,)),
                dma((n,)), dma((n,)),
                dma((plane,)), dma((plane,)),
            ],
            compiler_params=pltpu.CompilerParams(collective_id=0, has_side_effects=True),
        )(
            positions,
            jnp.transpose(frames, (1, 0, 2)),
            path_slot,
            path_count.reshape(1, n),
            path_order.reshape(-1, LANES),
            frame_rank.reshape(1, frames_n),
        )
        return forces, cv.reshape(2)

    return jax.shard_map(
        body,
        mesh=mesh,
        in_specs=(
            P(None, ("gx", "gy", "gz")),
            P(None, None, ("gy", "gz")),
            P(("gx", "gy", "gz"), None),
            P(),
            P(),
            P(),
        ),
        out_specs=(P(None, ("gx", "gy", "gz")), P()),
        check_vma=False,
    )
```

```python
import functools

import jax
import jax.numpy as jnp
from jax import lax
from jax.experimental import pallas as pl
from jax.experimental.pallas import tpu as pltpu
from jax.sharding import PartitionSpec as P

STRENGTH = 20.0
S_HOME = 0.5
KAPPA_S = 0.5
KAPPA_Z = 0.05
PAIR_SCALE = 0.02
WIDTH_SQ = 4.0
LANES = 128
MESH = pl.DeviceIdType.MESH
NT = (((1,), (1,)), ((), ()))
NN = (((1,), (0,)), ((), ()))


def three_parts(x):
    high = x.astype(jnp.bfloat16).astype(jnp.float32)
    rest = x - high
    middle = rest.astype(jnp.bfloat16).astype(jnp.float32)
    return high, middle, rest - middle


def dot(a, b, dims):
    return lax.dot_general(
        a.astype(jnp.bfloat16), b.astype(jnp.bfloat16), dims, preferred_element_type=jnp.float32
    )


def iota(shape, axis):
    return lax.broadcasted_iota(jnp.int32, shape, axis)


def kernel(
    sizes, tile, cpad,
    pos_hbm, frames_hbm, slot_hbm, count_hbm, order_hbm, rank_hbm,
    force_ref, cv_ref,
    frames, pos_ref, slot_ref, count_ref, order_ref, rank_ref, out1, in1, all2, all3, pair, cols,
    frames_sem, small_sem, sems1, sems2, sems3,
):
    nx, ny, nz = sizes
    plane = ny * nz
    n = nx * plane
    atoms = pos_ref.shape[1]
    slots = slot_ref.shape[1]
    order_rows = order_ref.shape[0]
    path = order_rows * LANES
    frames_n = frames.shape[1]
    block = frames.shape[2]
    parts = block // tile
    gx, gy, gz = lax.axis_index("gx"), lax.axis_index("gy"), lax.axis_index("gz")
    here = gy * nz + gz
    me = gx * plane + here

    def ring(at, size):
        return [at] + [jnp.where(at + step >= size, at + step - size, at + step) for step in range(1, size)]

    unrolled = n <= 64
    if unrolled:
        flat_peers = [(x, y, z) for x in ring(gx, nx) for y in ring(gy, ny) for z in ring(gz, nz)][:0:-1]
        near_peers = [(gx, y, z) for y in ring(gy, ny) for z in ring(gz, nz)][:0:-1]

    def everyone(fn):
        if unrolled:
            for device in flat_peers:
                fn(device)
            return

        def visit(step, carry):
            other = lax.rem(me + step, n)
            row = lax.rem(other, plane)
            fn((other // plane, row // nz, lax.rem(row, nz)))
            return carry

        lax.fori_loop(1, n, visit, 0)

    def neighbours(fn):
        if unrolled:
            for device in near_peers:
                fn(device)
            return

        def visit(step, carry):
            row = lax.rem(here + step, plane)
            fn((gx, row // nz, lax.rem(row, nz)))
            return carry

        lax.fori_loop(1, plane, visit, 0)

    def send(src, dst, sems, device):
        pltpu.make_async_remote_copy(
            src_ref=src, dst_ref=dst, send_sem=sems.at[0], recv_sem=sems.at[1],
            device_id=device, device_id_type=MESH).start()

    def whole(ref, count, sems):
        some = lax.rem(gx + 1, nx), gy, gz
        part = ref.at[pl.ds(0, count)]
        return pltpu.make_async_remote_copy(
            src_ref=part, dst_ref=part, send_sem=sems.at[0], recv_sem=sems.at[1],
            device_id=some, device_id_type=MESH)

    fetch = pltpu.make_async_copy(frames_hbm, frames, frames_sem)
    pairs = [(pos_hbm, pos_ref), (slot_hbm, slot_ref), (count_hbm, count_ref), (order_hbm, order_ref), (rank_hbm, rank_ref)]
    small = [pltpu.make_async_copy(src, dst, small_sem.at[i]) for i, (src, dst) in enumerate(pairs)]
    for copy in small:
        copy.start()
    fetch.start()

    barrier = pltpu.get_barrier_semaphore()
    everyone(lambda device: pl.semaphore_signal(barrier, inc=1, device_id=device, device_id_type=MESH))
    for copy in small:
        copy.wait()

    counts = count_ref[...]
    lane_n = iota(counts.shape, 1)
    offset = jnp.sum(jnp.where(lane_n < me, counts, 0).astype(jnp.float32), axis=1, keepdims=True).astype(jnp.int32)
    mine = jnp.sum(jnp.where(lane_n == me, counts, 0).astype(jnp.float32), axis=1, keepdims=True).astype(jnp.int32)
    k = iota((1, slots), 1)
    place = k + offset
    live_k = (k < mine).astype(jnp.float32)
    order = order_ref[...]
    table = jnp.concatenate([order // tile, lax.rem(order, tile)], axis=0).astype(jnp.float32)
    column = (iota((LANES, slots), 0) == lax.rem(place, LANES)).astype(jnp.float32)
    picked = dot(table, column, NN)
    row_hit = iota((order_rows, slots), 0) == place // LANES
    high_k = jnp.sum(jnp.where(row_hit, picked[:order_rows], 0.0), axis=0, keepdims=True)
    low_k = jnp.sum(jnp.where(row_hit, picked[order_rows:], 0.0), axis=0, keepdims=True)
    triple = jnp.concatenate(
        [high_k * live_k, low_k * live_k, live_k, jnp.zeros((5, slots), jnp.float32)], axis=0
    )
    slot_hit = (iota((atoms, slots), 0) == slot_ref[...]).astype(jnp.float32)
    per_atom = dot(triple, slot_hit, NT)
    live = per_atom[2:3]
    high = jnp.where(live > 0.5, per_atom[0:1].astype(jnp.int32), -1)
    low = per_atom[1:2].astype(jnp.int32)
    low_hit = (iota((tile, atoms), 0) == low).astype(jnp.bfloat16)

    pos = pos_ref[...]
    blocks = path // tile
    rows = blocks * cpad
    group = [pos, live]
    if cpad > 4:
        group.append(jnp.zeros((cpad - 4, atoms), jnp.float32))
    else:
        group = group * 2
    eight = jnp.concatenate(group, axis=0)
    high_hit = (iota((rows, atoms), 0) // cpad) == high
    sent = jnp.zeros((rows, tile), jnp.float32)
    for piece in three_parts(eight):
        wide = jnp.broadcast_to(piece[None], (rows // 8, 8, atoms)).reshape(rows, atoms)
        sent = sent + dot(jnp.where(high_hit, wide, 0.0), low_hit, NT)
    out1[...] = sent.reshape(plane, parts * cpad, tile)

    pl.semaphore_wait(barrier, n - 1)

    neighbours(lambda device: send(out1.at[device[1] * nz + device[2]], in1.at[here], sems1, device))
    in1[here] = out1[here]

    height = min(32, atoms)
    padded = jnp.concatenate([pos, jnp.zeros((5, atoms), jnp.float32)], axis=0)
    cols[...] = padded.T

    def pair_step(step, totals):
        at = pl.multiple_of(step * height, height)
        source = cols[pl.ds(at, height), :]
        diffs = [pos[c:c + 1] - source[:, c:c + 1] for c in range(3)]
        dist_sq = diffs[0] * diffs[0] + diffs[1] * diffs[1] + diffs[2] * diffs[2]
        weight = PAIR_SCALE * jnp.exp(-dist_sq / WIDTH_SQ)
        return tuple(
            total + jnp.sum((weight * diff).reshape(height // 8, 8, atoms), axis=0)
            for total, diff in zip(totals, diffs)
        )

    steps = atoms // height
    first = steps // 2
    totals = lax.fori_loop(0, first, pair_step, (jnp.zeros((8, atoms), jnp.float32),) * 3)

    whole(in1, plane - 1, sems1).wait_recv()
    fetch.wait()
    known = jnp.sum(in1[...], axis=0)
    squares = jnp.zeros((frames_n, tile), jnp.float32)
    for t in range(parts):
        part = jnp.zeros((frames_n, tile), jnp.float32)
        for c in range(3):
            row = t * cpad + c
            delta = known[row:row + 1] - frames[c, :, t * tile:(t + 1) * tile]
            part = part + delta * delta
        squares = squares + part * known[t * cpad + 3:t * cpad + 4]
    all2[me] = jnp.sum(squares.T, axis=0, keepdims=True)

    everyone(lambda device: send(all2.at[me], all2.at[me], sems2, device))

    totals = lax.fori_loop(first, steps, pair_step, totals)
    pair[...] = jnp.concatenate([jnp.sum(total, axis=0, keepdims=True) for total in totals], axis=0)

    whole(all2, n - 1, sems2).wait_recv()
    dist = jnp.sum(all2[...], axis=0) / path
    expo = -STRENGTH * dist
    top = jnp.max(expo, axis=1, keepdims=True)
    expd = jnp.exp(expo - top)
    total = jnp.sum(expd, axis=1, keepdims=True)
    weight = expd / total
    progress = rank_ref[...].astype(jnp.float32) / (frames_n - 1.0)
    s_value = jnp.sum(progress * weight, axis=1, keepdims=True)
    z_value = -(top + jnp.log(total)) / STRENGTH
    grads = (
        KAPPA_S * path * (s_value - S_HOME) * -STRENGTH * weight * (progress - s_value)
        + KAPPA_Z * path * z_value * weight
    )
    cv_ref[...] = jnp.concatenate([s_value, z_value], axis=1)
    down = jnp.broadcast_to(grads, (tile, frames_n)).T
    grads_sum = jnp.sum(grads, axis=1, keepdims=True)
    moved = []
    for t in range(parts):
        for c in range(3):
            pulled = jnp.sum(down * frames[c, :, t * tile:(t + 1) * tile], axis=0, keepdims=True)
            row = t * cpad + c
            moved.append(-(2.0 / path) * (grads_sum * known[row:row + 1] - pulled))
        moved.append(jnp.zeros((cpad - 3, tile), jnp.float32))
    all3[here] = jnp.concatenate(moved, axis=0)
    neighbours(lambda device: send(all3.at[here], all3.at[here], sems3, device))
    whole(in1, plane - 1, sems1).wait_send()
    whole(all2, n - 1, sems2).wait_send()
    whole(all3, plane - 1, sems3).wait_recv()
    full = all3[...].reshape(rows, tile)
    spread = jnp.zeros((rows, atoms), jnp.float32)
    for piece in three_parts(full):
        spread = spread + dot(piece, low_hit, NN)
    chosen = jnp.sum(jnp.where(high_hit, spread, 0.0).reshape(rows // 8, 8, atoms), axis=0)
    bias = chosen[0:3]
    if cpad == 4:
        bias = bias + chosen[4:7]
    force_ref[...] = pair[...] + bias
    whole(all3, plane - 1, sems3).wait_send()


def solution(mesh):
    sizes = tuple(mesh.shape[name] for name in ("gx", "gy", "gz"))

    def body(positions, frames, path_slot, path_count, path_order, frame_rank):
        plane = sizes[1] * sizes[2]
        n = sizes[0] * plane
        atoms = positions.shape[1]
        frames_n, _, block = frames.shape
        tile = min(LANES, block)
        parts = block // tile
        cpad = 4 if parts % 2 == 0 else 8
        dma = pltpu.SemaphoreType.DMA
        vmem = pl.BlockSpec(memory_space=pltpu.VMEM)
        forces, cv = pl.pallas_call(
            functools.partial(kernel, sizes, tile, cpad),
            out_shape=(
                pltpu.VMEM((3, atoms), jnp.float32),
                pltpu.VMEM((1, 2), jnp.float32),
            ),
            in_specs=[pl.BlockSpec(memory_space=pl.ANY)] * 6,
            out_specs=(vmem, vmem),
            scratch_shapes=[
                pltpu.VMEM((3, frames_n, block), jnp.float32),
                pltpu.VMEM((3, atoms), jnp.float32),
                pltpu.VMEM((1, path_slot.shape[1]), jnp.int32),
                pltpu.VMEM((1, n), jnp.int32),
                pltpu.VMEM((path_order.shape[0] // LANES, LANES), jnp.int32),
                pltpu.VMEM((1, frames_n), jnp.int32),
                pltpu.VMEM((plane, parts * cpad, tile), jnp.float32),
                pltpu.VMEM((plane, parts * cpad, tile), jnp.float32),
                pltpu.VMEM((n, 1, frames_n), jnp.float32),
                pltpu.VMEM((plane, parts * cpad, tile), jnp.float32),
                pltpu.VMEM((3, atoms), jnp.float32),
                pltpu.VMEM((atoms, 8), jnp.float32),
                dma, dma((5,)), dma((2,)), dma((2,)), dma((2,)),
            ],
            compiler_params=pltpu.CompilerParams(collective_id=0, has_side_effects=True),
        )(
            positions,
            jnp.transpose(frames, (1, 0, 2)),
            path_slot,
            path_count.reshape(1, n),
            path_order.reshape(-1, LANES),
            frame_rank.reshape(1, frames_n),
        )
        return forces, cv.reshape(2)

    return jax.shard_map(
        body,
        mesh=mesh,
        in_specs=(
            P(None, ("gx", "gy", "gz")),
            P(None, None, ("gy", "gz")),
            P(("gx", "gy", "gz"), None),
            P(),
            P(),
            P(),
        ),
        out_specs=(P(None, ("gx", "gy", "gz")), P()),
        check_vma=False,
    )
```
